128 devices in a mesh: grp: 16 (over x, z), tp: 8 (over y, core).
Axes of the slice: x: 4, y: 4, z: 4, core: 2. Of those that a mesh axis runs over, the one named last changes fastest.
Arguments:
- thinker_rows: bfloat16 [4096, 8192], P(('grp', 'tp')), may hold values from -6 to 6
- norm_gain: bfloat16 [8192], replicated, may hold values from 0.5 to 1.5
- w_query: bfloat16 [8192, 4096], P(None, 'tp'), may hold values from -0.0625 to 0.0625
- w_key: bfloat16 [8192, 1024], P(None, 'tp'), may hold values from -0.0625 to 0.0625
- w_value: bfloat16 [8192, 1024], P(None, 'tp'), may hold values from -0.0625 to 0.0625
- w_out: bfloat16 [4096, 8192], P('tp'), may hold values from -0.75 to 0.75
- cache_keys: bfloat16 [256, 320, 1024], P('grp', None, 'tp'), may hold values from -576 to 576
- cache_values: bfloat16 [256, 320, 1024], P('grp', None, 'tp'), may hold values from -6 to 6
- session_ids: int32 [16, 256], P('grp'), may hold values from 0 to 15, never falling along the last dimension, each value on 1 to 20 neighbouring positions
- cache_lens: int32 [16, 16], P('grp'), may hold values from 1 to 320, 3200 in all within a row
- owners: int32 [256, 1], P('grp'), may hold values from 0 to 15; in each aligned block of 16 rows (0 to 15, 16 to 31, ...) at most 2 rows name the same one
- talker_gain: bfloat16 [8192], replicated, may hold values from 0.5 to 1.5
- w_talker: bfloat16 [8192, 1024], P(None, 'tp'), may hold values from -0.0625 to 0.0625
Outputs:
- talker_rows: bfloat16 [10240, 1024], P('grp', 'tp')
The draws below stay inside these ranges and needn't reach their ends.
Inputs may be any that keep to these rules, and one draw needn't show every extreme that they name: `session_ids`: within a group the ids never fall; every one of the 16 sessions has 1 to 20 tokens and some session exactly 20. `cache_lens`: some session of every group has exactly 320 live slots. `owners`: of one group's 16 sessions at most 2 have the same owner, and some owner has exactly 2 of some group.
All inputs are finite; a program needn't handle non-finite values.
Results may differ from the reference program's by a relative error of at most 0.017.
The reference program's roundings to bfloat16 on the way count: a program that leaves them out, or rounds other values in their place, can miss the bound.
Values may be sent and summed in bfloat16 or wider, within the bound.
No kernel may reach another device: no remote copies, remote signals or barrier semaphores. Data moves between devices by JAX's collectives and lax.ppermute only.
A program may use at most 128 MiB of HBM per device.

```python
import math
import jax
import jax.numpy as jnp
import numpy as np
from jax import lax

D = 8192
HEADS = 32
KV_HEADS = 8
HEAD_DIM = 128
TW = 1024
SESS = 16
CACHE = 320
CAPS = 2
TOK = 256
GQA = 4
MOST = 20
TOKENS = 4096
SESSIONS = 256
TROWS = 10240
N_GRP = 16


def draw_cache_keys(key, part):
    base = jnp.clip(jax.random.normal(key, (SESSIONS, CACHE, KV_HEADS * HEAD_DIM), jnp.float32), -6.0, 6.0)
    return base.astype(jnp.bfloat16)


def levels(key, shape, shards, low, top_value):
    loudness = 1.0
    for dim, shards_of in shards:
        draws = jax.random.uniform(jax.random.fold_in(jax.random.fold_in(key, 6), dim), (shards_of,), jnp.float32, low / len(shards), top_value / len(shards))
        loudness = loudness * jnp.repeat(jnp.exp(draws), shape[dim] // shards_of).reshape((-1,) + (1,) * (len(shape) - 1 - dim))
    return loudness


def split_up(amount, total, most, lean):
    portions = [(1 << 20) // math.isqrt(rank ** lean) + 1 for rank in range(2, amount + 1)]
    surplus, holding = total - most - (amount - 1), [1] * (amount - 1)
    while surplus > 0:
        movable = [i for i in range(amount - 1) if holding[i] < most]
        whole, remaining = sum([portions[i] for i in movable]), surplus
        for i in movable:
            more = min(most - holding[i], max(1, remaining * portions[i] // whole), surplus)
            holding[i] = holding[i] + more
            surplus = surplus - more
    return np.array([most] + holding)


def uneven(own_key, number_of, total, most, skew):
    if number_of == 2:
        one = jax.random.randint(own_key, (), max(1, total - most), min(most, total - 1) + 1)
        return jnp.stack([one, total - one])
    lengths = jnp.asarray(split_up(number_of, total, most, skew), jnp.int32)
    pairs = (number_of - 1) // 2
    donor, taker = lengths[1:1 + 2 * pairs:2], lengths[2:2 + 2 * pairs:2]
    margin = jnp.minimum(donor - 1, most - taker)
    passed = jax.random.randint(jax.random.fold_in(own_key, 1), (pairs,), 0, 1 << 20) % (margin + 1)
    lengths = lengths.at[1:1 + 2 * pairs:2].set(donor - passed).at[2:2 + 2 * pairs:2].set(taker + passed)
    return lengths[jax.random.permutation(jax.random.fold_in(own_key, 2), number_of)]


def assign_block(own_key, own, number, rows, number_of, top, bound, skew):
    order = jax.random.permutation(own_key, number_of)
    heavy_load, ordinary = load_shares(number_of, rows * top, bound, skew, True), load_shares(number_of, rows * top, bound, skew, False)
    places = jnp.arange(number_of)

    def named(lengths, offset_by):
        used = int((lengths > 0).sum())
        fixed = max(1, used // 4)
        moved = fixed + (places - fixed + offset_by * (used - fixed)) % max(1, number_of - fixed)
        return jnp.zeros((number_of,), jnp.int32).at[order[jnp.where(places < fixed, places, moved)]].set(jnp.asarray(lengths, jnp.int32))

    lengths = jnp.where(number % 4 == 0, named(heavy_load, number // 4), named(ordinary, number - number // 4 - 1))
    mixed = jax.random.permutation(jax.random.fold_in(own, 3), number_of)
    source_of, sink = mixed[0:number_of // 2 * 2:2], mixed[1:number_of // 2 * 2:2]
    margin = jnp.minimum(lengths[source_of] - 1, bound - lengths[sink]) // 2
    margin = jnp.where((source_of == order[0]) | (sink == order[0]) | (lengths[sink] == 0), 0, jnp.maximum(margin, 0))
    moved = jax.random.randint(jax.random.fold_in(own, 4), (number_of // 2,), 0, 1 << 20) % (margin + 1)
    lengths = lengths.at[source_of].add(-moved).at[sink].add(moved)
    members = jnp.searchsorted(jnp.cumsum(lengths), jnp.arange(rows * top), side="right").astype(jnp.int32)
    listing = members.reshape(top, rows).T
    listing = listing[jax.random.permutation(jax.random.fold_in(own, 1), rows)]
    offset_by = jax.random.randint(jax.random.fold_in(own, 2), (rows, 1), 0, top)
    return jnp.take_along_axis(listing, (jnp.arange(top)[None, :] + offset_by) % top, axis=1)


def load_shares(count, total, most, skew, full):
    portions = [(1 << 20) // math.isqrt(rank ** skew) + 1 for rank in range(1, count + 1)]
    largest = most if full else min(most, max(-(-total // count), total * portions[0] // sum(portions)))
    least = 1 if total - largest >= count - 1 else 0
    holding, rest = [largest] + [least] * (count - 1), total - largest - least * (count - 1)
    while rest > 0:
        free = [i for i in range(1, count) if holding[i] < largest] or [i for i in range(1, count) if holding[i] < most]
        pool, remaining = sum([portions[i] for i in free]), rest
        for i in free:
            addition = min(most - holding[i], max(1, remaining * portions[i] // pool), rest)
            holding[i] = holding[i] + addition
            rest = rest - addition
    return np.array(holding)


def gaussian(stream_key, extent, deviation, bound, shards=(), kind=jnp.bfloat16):
    array = jax.random.normal(stream_key, extent, jnp.float32) * deviation
    if len(shards) > 0:
        array = levels(stream_key, extent, shards, -0.22, 0.18) * array
    return jnp.clip(array, min=-bound, max=bound).astype(kind)


def setup_inputs(seed: int = 0) -> dict:
    key_of = jax.random.split(jax.random.key(seed), 14)
    thinker_rows = gaussian(key_of[0], (TOKENS, D), 1.0, 6.0, ((0, 128),))
    norm_gain = jnp.clip(1.0 + 0.1 * jax.random.normal(key_of[1], (D,), jnp.float32), 0.5, 1.5).astype(jnp.bfloat16)
    w_query = gaussian(key_of[2], (D, HEADS * HEAD_DIM), D ** -0.5, 0.0625, ((1, 8),))
    w_key = gaussian(key_of[3], (D, KV_HEADS * HEAD_DIM), D ** -0.5, 0.0625, ((1, 8),))
    w_value = gaussian(key_of[4], (D, KV_HEADS * HEAD_DIM), D ** -0.5, 0.0625, ((1, 8),))
    w_out = gaussian(key_of[5], (HEADS * HEAD_DIM, D), (HEADS * HEAD_DIM // 64) ** -0.5, 0.75, ((0, 8),))
    cache_keys = draw_cache_keys(jax.random.fold_in(key_of[13], 71), 0)
    cache_values = gaussian(key_of[7], (SESSIONS, CACHE, KV_HEADS * HEAD_DIM), 1.0, 6.0, ((0, 16), (2, 8)))
    session_ids = jax.vmap(lambda own: jnp.searchsorted(jnp.cumsum(uneven(own, SESS, TOK, MOST, 1)), jnp.arange(TOK), side="right"))(jax.random.split(key_of[8], N_GRP)).reshape((N_GRP, TOK)).astype(jnp.int32)
    cache_lens = jax.vmap(lambda own: uneven(own, SESS, SESS * CACHE * 5 // 8, CACHE, 1))(jax.random.split(key_of[9], N_GRP)).reshape((N_GRP, SESS)).astype(jnp.int32)
    owners_keys = jax.random.split(jax.random.fold_in(key_of[10], 1), SESSIONS // SESS)
    owners_turns = jax.random.permutation(jax.random.fold_in(key_of[10], 3), SESSIONS // SESS)
    owners = jax.vmap(lambda own, number: assign_block(jax.random.fold_in(key_of[10], 2), own, number, SESS, N_GRP, 1, CAPS, 2))(owners_keys, owners_turns).reshape((SESSIONS, 1))
    talker_gain = jnp.clip(1.0 + 0.1 * jax.random.normal(key_of[11], (D,), jnp.float32), 0.5, 1.5).astype(jnp.bfloat16)
    w_talker = gaussian(key_of[12], (D, TW), D ** -0.5, 0.0625, ((1, 8),))
    return {"thinker_rows": thinker_rows, "norm_gain": norm_gain, "w_query": w_query, "w_key": w_key, "w_value": w_value, "w_out": w_out, "cache_keys": cache_keys, "cache_values": cache_values, "session_ids": session_ids, "cache_lens": cache_lens, "owners": owners, "talker_gain": talker_gain, "w_talker": w_talker}


EPSILON = 1e-06

def rms_scaled(values, weights):
    floats = values.astype(jnp.float32)
    mean_square = lax.optimization_barrier(jnp.mean(floats * floats, axis=-1, keepdims=True))
    return (floats * lax.rsqrt(mean_square + EPSILON) * weights.astype(jnp.float32)).astype(jnp.bfloat16)

def slot_tables(session_row, owner_row):
    session_range = jnp.arange(SESS, dtype=jnp.int32)
    member = (session_row[:, None] == session_range[None, :]).astype(jnp.int32)
    counts = lax.optimization_barrier(jnp.sum(member, axis=0))
    starts = jnp.cumsum(counts) - counts
    first_row = lax.optimization_barrier(jnp.sum(member * starts[None, :], axis=1))
    position = jnp.arange(session_row.shape[0], dtype=jnp.int32) - first_row
    earlier = (owner_row[:, None] == owner_row[None, :]) & (session_range[None, :] < session_range[:, None])
    owner_rank = lax.optimization_barrier(jnp.sum(earlier.astype(jnp.int32), axis=1))
    owner_slot = owner_row * CAPS + owner_rank
    destination = lax.optimization_barrier(jnp.sum(member * owner_slot[None, :], axis=1)) * MOST + position
    slot_index = session_row * MOST + position
    return (counts, slot_index, destination)

def attend(q_slots, k_slots, v_slots, cache_k, cache_v, live_lens, counts):
    score_scale = HEAD_DIM ** (-0.5)
    cached = jnp.einsum('smkgd,sckd->skgmc', q_slots.astype(jnp.float32), cache_k.astype(jnp.float32)) * score_scale
    fresh = jnp.einsum('smkgd,snkd->skgmn', q_slots.astype(jnp.float32), k_slots.astype(jnp.float32)) * score_scale
    live_cache = jnp.arange(cache_k.shape[1], dtype=jnp.int32)[None, :] < live_lens[:, None]
    places = jnp.arange(MOST, dtype=jnp.int32)
    causal = places[None, :] <= places[:, None]
    live_fresh = causal[None, :, :] & (places[None, None, :] < counts[:, None, None])
    cached = jnp.where(live_cache[:, None, None, None, :], cached, -1e+30)
    fresh = jnp.where(live_fresh[:, None, None, :, :], fresh, -1e+30)
    highest = jnp.maximum(lax.optimization_barrier(jnp.max(cached, axis=-1)), lax.optimization_barrier(jnp.max(fresh, axis=-1)))
    exp_cached = jnp.exp(cached - highest[..., None])
    exp_fresh = jnp.exp(fresh - highest[..., None])
    denominator = lax.optimization_barrier(jnp.sum(exp_cached, axis=-1)) + lax.optimization_barrier(jnp.sum(exp_fresh, axis=-1))
    weight_cached = (exp_cached / denominator[..., None]).astype(jnp.bfloat16)
    weight_fresh = (exp_fresh / denominator[..., None]).astype(jnp.bfloat16)
    mixed = jnp.einsum('skgmc,sckd->smkgd', weight_cached.astype(jnp.float32), cache_v.astype(jnp.float32))
    mixed = mixed + jnp.einsum('skgmn,snkd->smkgd', weight_fresh.astype(jnp.float32), v_slots.astype(jnp.float32))
    return mixed.astype(jnp.bfloat16)

def reference(thinker_rows, norm_gain, w_query, w_key, w_value, w_out, cache_keys, cache_values, session_ids, cache_lens, owners, talker_gain, w_talker):
    slot_count = SESS * MOST
    head_width = GQA * HEAD_DIM

    def one_group(operands):
        thinker, session_row, length_row, owner_row, keys_group, values_group = operands
        normed = rms_scaled(thinker, norm_gain)
        query = jnp.dot(normed, w_query, preferred_element_type=jnp.float32).astype(jnp.bfloat16)
        key_new = jnp.dot(normed, w_key, preferred_element_type=jnp.float32).astype(jnp.bfloat16)
        value_new = jnp.dot(normed, w_value, preferred_element_type=jnp.float32).astype(jnp.bfloat16)
        counts, slot_index, destination = slot_tables(session_row, owner_row)
        placing = (slot_index[None, :] == jnp.arange(slot_count, dtype=jnp.int32)[:, None]).astype(jnp.bfloat16)
        q_slots = jnp.dot(placing, query, preferred_element_type=jnp.float32).astype(jnp.bfloat16)
        k_slots = jnp.dot(placing, key_new, preferred_element_type=jnp.float32).astype(jnp.bfloat16)
        v_slots = jnp.dot(placing, value_new, preferred_element_type=jnp.float32).astype(jnp.bfloat16)
        mixed = attend(q_slots.reshape(SESS, MOST, KV_HEADS, GQA, HEAD_DIM), k_slots.reshape(SESS, MOST, KV_HEADS, HEAD_DIM), v_slots.reshape(SESS, MOST, KV_HEADS, HEAD_DIM), keys_group, values_group, length_row, counts)
        attention_rows = jnp.dot(placing.T, mixed.reshape(slot_count, HEADS * HEAD_DIM), preferred_element_type=jnp.float32).astype(jnp.bfloat16)
        head_total = jnp.zeros((TOK, D), jnp.float32)
        for kv_index in range(KV_HEADS):
            lower = kv_index * head_width
            partial_sum = jnp.dot(attention_rows[:, lower:lower + head_width], w_out[lower:lower + head_width], preferred_element_type=jnp.float32).astype(jnp.bfloat16)
            head_total = head_total + partial_sum.astype(jnp.float32)
        hidden = (thinker.astype(jnp.float32) + head_total).astype(jnp.bfloat16)
        routing = (destination[None, :] == jnp.arange(N_GRP * CAPS * MOST, dtype=jnp.int32)[:, None]).astype(jnp.bfloat16)
        return jnp.dot(routing, hidden, preferred_element_type=jnp.float32).astype(jnp.bfloat16).reshape(N_GRP, CAPS * MOST, D)
    sent = lax.map(one_group, (thinker_rows.reshape(N_GRP, TOK, D), session_ids, cache_lens, owners.reshape(N_GRP, SESS), cache_keys.reshape(N_GRP, SESS, CACHE, KV_HEADS, HEAD_DIM), cache_values.reshape(N_GRP, SESS, CACHE, KV_HEADS, HEAD_DIM)))
    received = jnp.transpose(sent, (1, 0, 2, 3))

    def one_owner(block_rows):
        return jnp.dot(rms_scaled(block_rows.reshape(-1, D), talker_gain), w_talker, preferred_element_type=jnp.float32).astype(jnp.bfloat16)
    return lax.map(one_owner, received).reshape(TROWS, TW)
```

```python
import jax
import jax.numpy as jnp
from jax import lax
from jax.sharding import PartitionSpec as P

HEAD_DIM = 128
SESS = 16
CAPS = 2
GQA = 4
MOST = 20


EPSILON = 1e-06


def rms_scaled(values, weights):
    floats = values.astype(jnp.float32)
    mean_square = jnp.mean(floats * floats, axis=-1, keepdims=True)
    return (floats * lax.rsqrt(mean_square + EPSILON) * weights.astype(jnp.float32)).astype(
        jnp.bfloat16
    )


def slot_tables(session_row, owner_row):
    session_range = jnp.arange(SESS, dtype=jnp.int32)
    member = (session_row[:, None] == session_range[None, :]).astype(jnp.int32)
    counts = jnp.sum(member, axis=0)
    starts = jnp.cumsum(counts) - counts
    first_row = jnp.sum(member * starts[None, :], axis=1)
    position = jnp.arange(session_row.shape[0], dtype=jnp.int32) - first_row
    earlier = (owner_row[:, None] == owner_row[None, :]) & (
        session_range[None, :] < session_range[:, None]
    )
    owner_rank = jnp.sum(earlier.astype(jnp.int32), axis=1)
    owner_slot = owner_row * CAPS + owner_rank
    destination = jnp.sum(member * owner_slot[None, :], axis=1) * MOST + position
    slot_index = session_row * MOST + position
    return (counts, slot_index, destination)


def attend(q_slots, k_slots, v_slots, cache_k, cache_v, live_lens, counts):
    score_scale = HEAD_DIM ** (-0.5)
    cached = (
        jnp.einsum("smkgd,sckd->skgmc", q_slots, cache_k, preferred_element_type=jnp.float32)
        * score_scale
    )
    fresh = (
        jnp.einsum("smkgd,snkd->skgmn", q_slots, k_slots, preferred_element_type=jnp.float32)
        * score_scale
    )
    live_cache = jnp.arange(cache_k.shape[1], dtype=jnp.int32)[None, :] < live_lens[:, None]
    places = jnp.arange(MOST, dtype=jnp.int32)
    causal = places[None, :] <= places[:, None]
    live_fresh = causal[None, :, :] & (places[None, None, :] < counts[:, None, None])
    cached = jnp.where(live_cache[:, None, None, None, :], cached, -1e30)
    fresh = jnp.where(live_fresh[:, None, None, :, :], fresh, -1e30)
    highest = jnp.maximum(jnp.max(cached, axis=-1), jnp.max(fresh, axis=-1))
    exp_cached = jnp.exp(cached - highest[..., None])
    exp_fresh = jnp.exp(fresh - highest[..., None])
    denominator = jnp.sum(exp_cached, axis=-1) + jnp.sum(exp_fresh, axis=-1)
    weight_cached = (exp_cached / denominator[..., None]).astype(jnp.bfloat16)
    weight_fresh = (exp_fresh / denominator[..., None]).astype(jnp.bfloat16)
    mixed = jnp.einsum(
        "skgmc,sckd->smkgd", weight_cached, cache_v, preferred_element_type=jnp.float32
    )
    mixed = mixed + jnp.einsum(
        "skgmn,snkd->smkgd", weight_fresh, v_slots, preferred_element_type=jnp.float32
    )
    return mixed.astype(jnp.bfloat16)


def on_device(
    thinker_rows,
    norm_gain,
    w_query,
    w_key,
    w_value,
    w_out,
    cache_keys,
    cache_values,
    session_ids,
    cache_lens,
    owners,
    talker_gain,
    w_talker,
):
    kv_local = w_key.shape[1] // HEAD_DIM
    head_width = GQA * HEAD_DIM
    slot_count = SESS * MOST
    owner_count = lax.axis_size("grp")
    gathered = lax.all_gather(thinker_rows, "tp", axis=0, tiled=True)
    normed = rms_scaled(gathered, norm_gain)
    query = jnp.dot(normed, w_query, preferred_element_type=jnp.float32).astype(jnp.bfloat16)
    key_new = jnp.dot(normed, w_key, preferred_element_type=jnp.float32).astype(jnp.bfloat16)
    value_new = jnp.dot(normed, w_value, preferred_element_type=jnp.float32).astype(jnp.bfloat16)
    counts, slot_index, destination = slot_tables(session_ids[0], owners[:, 0])
    placing = (slot_index[None, :] == jnp.arange(slot_count, dtype=jnp.int32)[:, None]).astype(
        jnp.bfloat16
    )
    q_slots = jnp.dot(placing, query, preferred_element_type=jnp.float32).astype(jnp.bfloat16)
    k_slots = jnp.dot(placing, key_new, preferred_element_type=jnp.float32).astype(jnp.bfloat16)
    v_slots = jnp.dot(placing, value_new, preferred_element_type=jnp.float32).astype(jnp.bfloat16)
    mixed = attend(
        q_slots.reshape(SESS, MOST, kv_local, GQA, HEAD_DIM),
        k_slots.reshape(SESS, MOST, kv_local, HEAD_DIM),
        v_slots.reshape(SESS, MOST, kv_local, HEAD_DIM),
        cache_keys.reshape(SESS, cache_keys.shape[1], kv_local, HEAD_DIM),
        cache_values.reshape(SESS, cache_values.shape[1], kv_local, HEAD_DIM),
        cache_lens[0],
        counts,
    )
    attention_rows = lax.dot_general(
        placing,
        mixed.reshape(slot_count, kv_local * head_width),
        (((0,), (0,)), ((), ())),
        preferred_element_type=jnp.float32,
    ).astype(jnp.bfloat16)
    routing = (
        destination[None, :] == jnp.arange(owner_count * CAPS * MOST, dtype=jnp.int32)[:, None]
    ).astype(jnp.bfloat16)
    partial_sum = jnp.dot(attention_rows, w_out, preferred_element_type=jnp.float32).astype(
        jnp.bfloat16
    )
    head_total = partial_sum.astype(jnp.float32)
    summed = lax.psum_scatter(
        head_total.astype(jnp.bfloat16), "tp", scatter_dimension=0, tiled=True
    ).astype(jnp.float32)
    hidden_local = (thinker_rows.astype(jnp.float32) + summed).astype(jnp.bfloat16)
    hidden = lax.all_gather(hidden_local, "tp", axis=0, tiled=True)
    talker_here = jnp.dot(
        rms_scaled(hidden, talker_gain), w_talker, preferred_element_type=jnp.float32
    ).astype(jnp.bfloat16)
    outgoing = (
        jnp.dot(routing, talker_here, preferred_element_type=jnp.float32)
        .astype(jnp.bfloat16)
        .reshape(owner_count, CAPS * MOST, w_talker.shape[1])
    )
    arrived = lax.all_to_all(outgoing, "grp", split_axis=0, concat_axis=0, tiled=True)
    return arrived.reshape(owner_count * CAPS * MOST, w_talker.shape[1])


def solution(mesh):
    return jax.shard_map(
        on_device,
        mesh=mesh,
        in_specs=(
            P(("grp", "tp"), None),
            P(),
            P(None, "tp"),
            P(None, "tp"),
            P(None, "tp"),
            P("tp", None),
            P("grp", None, "tp"),
            P("grp", None, "tp"),
            P("grp", None),
            P("grp", None),
            P("grp", None),
            P(),
            P(None, "tp"),
        ),
        out_specs=P("grp", "tp"),
        check_vma=False,
    )
```

```python
import jax
import jax.numpy as jnp
from jax import lax
from jax.sharding import Mesh, PartitionSpec as P

HEAD_DIM = 128
SESS = 16
CAPS = 2
GQA = 4
MOST = 20


EPSILON = 1e-06


def rms_scaled(values, weights):
    floats = values.astype(jnp.float32)
    mean_square = jnp.mean(floats * floats, axis=-1, keepdims=True)
    return (floats * lax.rsqrt(mean_square + EPSILON) * weights.astype(jnp.float32)).astype(
        jnp.bfloat16
    )


def slot_tables(session_row, owner_row):
    session_range = jnp.arange(SESS, dtype=jnp.int32)
    member = (session_row[:, None] == session_range[None, :]).astype(jnp.int32)
    counts = jnp.sum(member, axis=0)
    starts = jnp.cumsum(counts) - counts
    first_row = jnp.sum(member * starts[None, :], axis=1)
    position = jnp.arange(session_row.shape[0], dtype=jnp.int32) - first_row
    earlier = (owner_row[:, None] == owner_row[None, :]) & (
        session_range[None, :] < session_range[:, None]
    )
    owner_rank = jnp.sum(earlier.astype(jnp.int32), axis=1)
    owner_slot = owner_row * CAPS + owner_rank
    destination = jnp.sum(member * owner_slot[None, :], axis=1) * MOST + position
    slot_index = session_row * MOST + position
    return (counts, slot_index, destination)


def attend(q_slots, k_slots, v_slots, cache_k, cache_v, live_lens, counts):
    score_scale = HEAD_DIM ** (-0.5)
    cached = (
        jnp.einsum("smkgd,sckd->skgmc", q_slots, cache_k, preferred_element_type=jnp.float32)
        * score_scale
    )
    fresh = (
        jnp.einsum("smkgd,snkd->skgmn", q_slots, k_slots, preferred_element_type=jnp.float32)
        * score_scale
    )
    live_cache = jnp.arange(cache_k.shape[1], dtype=jnp.int32)[None, :] < live_lens[:, None]
    places = jnp.arange(MOST, dtype=jnp.int32)
    causal = places[None, :] <= places[:, None]
    live_fresh = causal[None, :, :] & (places[None, None, :] < counts[:, None, None])
    cached = jnp.where(live_cache[:, None, None, None, :], cached, -1e30)
    fresh = jnp.where(live_fresh[:, None, None, :, :], fresh, -1e30)
    highest = jnp.maximum(jnp.max(cached, axis=-1), jnp.max(fresh, axis=-1))
    exp_cached = jnp.exp(cached - highest[..., None])
    exp_fresh = jnp.exp(fresh - highest[..., None])
    denominator = jnp.sum(exp_cached, axis=-1) + jnp.sum(exp_fresh, axis=-1)
    weight_cached = (exp_cached / denominator[..., None]).astype(jnp.bfloat16)
    weight_fresh = (exp_fresh / denominator[..., None]).astype(jnp.bfloat16)
    mixed = jnp.einsum(
        "skgmc,sckd->smkgd", weight_cached, cache_v, preferred_element_type=jnp.float32
    )
    mixed = mixed + jnp.einsum(
        "skgmn,snkd->smkgd", weight_fresh, v_slots, preferred_element_type=jnp.float32
    )
    return mixed.astype(jnp.bfloat16)


def shift(values, axis, step):
    size = lax.axis_size(axis)
    return lax.ppermute(values, axis, [(i, (i + step) % size) for i in range(size)])


def pick(values, index):
    return lax.dynamic_index_in_dim(values, index, 0, keepdims=False)


def exchange(values, axis):
    here = lax.axis_index(axis)
    return [pick(values, here)] + [
        shift(pick(values, (here + d) % 4), axis, d) for d in (1, 3, 2)
    ]


def in_order(parts, sources, shape):
    held = jnp.zeros((len(parts),) + shape, parts[0].dtype)
    for part, source in zip(parts, sources):
        held = lax.dynamic_update_index_in_dim(held, part, source, 0)
    return held


def all_to_all_4(values, axis):
    here = lax.axis_index(axis)
    got = exchange(values, axis)
    return in_order(got, [(here - d) % 4 for d in (0, 1, 3, 2)], values.shape[1:])


def gather_4(values, axis):
    here = lax.axis_index(axis)
    half = values.shape[0] // 2
    left, right = shift(values, axis, 1), shift(values, axis, -1)
    far = jnp.concatenate([shift(left[:half], axis, 1), shift(right[half:], axis, -1)], 0)
    return [values, left, right, far], [(here - d) % 4 for d in (0, 1, 3, 2)]


def gather_rows(rows):
    y, core = lax.axis_index("y"), lax.axis_index("core")
    blocks, sources = gather_4(rows, "y")
    twins = [shift(block, "core", 1) for block in blocks]
    every = jnp.zeros((8,) + rows.shape, rows.dtype)
    for block, twin, source in zip(blocks, twins, sources):
        every = lax.dynamic_update_index_in_dim(every, block, source * 2 + core, 0)
        every = lax.dynamic_update_index_in_dim(every, twin, source * 2 + 1 - core, 0)
    return every.reshape(-1, rows.shape[1])


def talker_rows_of(w_talker):
    core = lax.axis_index("core")
    group = lax.axis_index("x") * 4 + lax.axis_index("z")
    width = w_talker.shape[1]
    depth = w_talker.shape[0] // 8
    piece = depth // 16
    mine = lax.dynamic_index_in_dim(
        w_talker.reshape(4, 2, 16, piece, width), group, 2, keepdims=False
    )
    kept = lax.dynamic_index_in_dim(mine, core, 1, keepdims=False)
    twin = shift(lax.dynamic_index_in_dim(mine, 1 - core, 1, keepdims=False), "core", 1)
    both = jnp.where(core == 0, jnp.stack([kept, twin], 1), jnp.stack([twin, kept], 1))
    across = all_to_all_4(both, "y").reshape(8, piece, width)
    strip = jnp.transpose(across, (1, 0, 2)).reshape(piece, 8 * width)
    parts, sources = gather_4(strip, "z")
    strip = in_order(parts, sources, strip.shape).reshape(4 * piece, 8 * width)
    parts, sources = gather_4(strip, "x")
    return in_order(parts, sources, strip.shape).reshape(depth, 8 * width)


def on_device(
    thinker_rows,
    norm_gain,
    w_query,
    w_key,
    w_value,
    w_out,
    cache_keys,
    cache_values,
    session_ids,
    cache_lens,
    owners,
    talker_gain,
    w_talker,
):
    model_width = thinker_rows.shape[1]
    kv_local = w_key.shape[1] // HEAD_DIM
    head_width = GQA * HEAD_DIM
    slot_count = SESS * MOST
    owner_count = 16
    y, core = lax.axis_index("y"), lax.axis_index("core")
    member = y * 2 + core
    share = model_width // 8
    gathered = gather_rows(thinker_rows)
    talker_block = talker_rows_of(w_talker)
    normed = rms_scaled(gathered, norm_gain)
    query = jnp.dot(normed, w_query, preferred_element_type=jnp.float32).astype(jnp.bfloat16)
    key_new = jnp.dot(normed, w_key, preferred_element_type=jnp.float32).astype(jnp.bfloat16)
    value_new = jnp.dot(normed, w_value, preferred_element_type=jnp.float32).astype(jnp.bfloat16)
    counts, slot_index, destination = slot_tables(session_ids[0], owners[:, 0])
    placing = (slot_index[None, :] == jnp.arange(slot_count, dtype=jnp.int32)[:, None]).astype(
        jnp.bfloat16
    )
    q_slots = jnp.dot(placing, query, preferred_element_type=jnp.float32).astype(jnp.bfloat16)
    k_slots = jnp.dot(placing, key_new, preferred_element_type=jnp.float32).astype(jnp.bfloat16)
    v_slots = jnp.dot(placing, value_new, preferred_element_type=jnp.float32).astype(jnp.bfloat16)
    mixed = attend(
        q_slots.reshape(SESS, MOST, kv_local, GQA, HEAD_DIM),
        k_slots.reshape(SESS, MOST, kv_local, HEAD_DIM),
        v_slots.reshape(SESS, MOST, kv_local, HEAD_DIM),
        cache_keys.reshape(SESS, cache_keys.shape[1], kv_local, HEAD_DIM),
        cache_values.reshape(SESS, cache_values.shape[1], kv_local, HEAD_DIM),
        cache_lens[0],
        counts,
    )
    attention_rows = lax.dot_general(
        placing,
        mixed.reshape(slot_count, kv_local * head_width),
        (((0,), (0,)), ((), ())),
        preferred_element_type=jnp.float32,
    ).astype(jnp.bfloat16)
    routing = (
        destination[None, :] == jnp.arange(owner_count * CAPS * MOST, dtype=jnp.int32)[:, None]
    ).astype(jnp.bfloat16)
    partial_sum = jnp.dot(attention_rows, w_out, preferred_element_type=jnp.float32).astype(
        jnp.bfloat16
    )
    def block_of(chip, which):
        return lax.dynamic_slice(
            partial_sum, (0, ((chip % 4) * 2 + which) * share), (partial_sum.shape[0], share)
        )

    def joined(chip):
        other = shift(block_of(chip, 1 - core), "core", 1)
        return block_of(chip, core).astype(jnp.float32) + other.astype(jnp.float32)

    half = partial_sum.shape[0] // 2
    far = joined(y + 2).astype(jnp.bfloat16)
    ahead, behind = shift(far[:half], "y", 1), shift(far[half:], "y", -1)
    none = jnp.zeros((half, share), jnp.float32)
    to_next = joined(y + 1) + jnp.concatenate([ahead.astype(jnp.float32), none], 0)
    to_last = joined(y + 3) + jnp.concatenate([none, behind.astype(jnp.float32)], 0)
    from_last = shift(to_next.astype(jnp.bfloat16), "y", 1)
    from_next = shift(to_last.astype(jnp.bfloat16), "y", -1)
    own = lax.dynamic_slice(gathered, (0, member * share), (gathered.shape[0], share))
    hidden = (
        own.astype(jnp.float32)
        + joined(y)
        + from_last.astype(jnp.float32)
        + from_next.astype(jnp.float32)
    ).astype(jnp.bfloat16)
    floats = hidden.astype(jnp.float32)
    squares = jnp.sum(floats * floats, axis=1)
    squares = squares + shift(squares, "core", 1)
    squares = squares + shift(squares, "y", 1) + shift(squares, "y", 2) + shift(squares, "y", 3)
    scale = lax.rsqrt(squares / model_width + EPSILON)
    gain = lax.dynamic_slice(talker_gain, (member * share,), (share,)).astype(jnp.float32)
    product = jnp.dot(
        (floats * gain[None, :]).astype(jnp.bfloat16),
        talker_block,
        preferred_element_type=jnp.float32,
    ).reshape(-1, 4, 2, w_talker.shape[1])
    kept = lax.dynamic_index_in_dim(product, core, 2, keepdims=False)
    sent = lax.dynamic_index_in_dim(product, 1 - core, 2, keepdims=False)
    kept = kept + shift(sent.astype(jnp.bfloat16), "core", 1).astype(jnp.float32)
    kept = jnp.transpose(kept, (1, 0, 2))
    got = exchange(kept.astype(jnp.bfloat16), "y")
    total = pick(kept, y) + sum(part.astype(jnp.float32) for part in got[1:])
    talker_here = (total * scale[:, None]).astype(jnp.bfloat16)
    outgoing = (
        jnp.dot(routing, talker_here, preferred_element_type=jnp.float32)
        .astype(jnp.bfloat16)
        .reshape(4, 4, CAPS * MOST, w_talker.shape[1])
    )
    arrived = jnp.transpose(all_to_all_4(outgoing, "x"), (1, 0, 2, 3))
    arrived = jnp.transpose(all_to_all_4(arrived, "z"), (1, 0, 2, 3))
    return arrived.reshape(owner_count * CAPS * MOST, w_talker.shape[1])


def solution(mesh):
    grp, tp = ("x", "z"), ("y", "core")
    return jax.shard_map(
        on_device,
        mesh=Mesh(mesh.devices.reshape(4, 4, 4, 2), grp + tp),
        in_specs=(
            P(grp + tp, None),
            P(),
            P(None, tp),
            P(None, tp),
            P(None, tp),
            P(tp, None),
            P(grp, None, tp),
            P(grp, None, tp),
            P(grp, None),
            P(grp, None),
            P(grp, None),
            P(),
            P(None, tp),
        ),
        out_specs=P(grp, tp),
        check_vma=False,
    )
```

```python
import functools

import jax
import jax.numpy as jnp
from jax import lax
from jax.experimental import pallas as pl
from jax.experimental.pallas import tpu as pltpu
from jax.sharding import Mesh, PartitionSpec as P

HEAD_DIM = 128
SESS = 16
CACHE = 320
CAPS = 2
GQA = 4
MOST = 20
ROOM = 32
KEYS = 384

EPSILON = 1e-06

VMEM = pl.BlockSpec(memory_space=pltpu.VMEM)
SMEM = pl.BlockSpec(memory_space=pltpu.SMEM)
ANY = pl.BlockSpec(memory_space=pl.ANY)


def call(kernel, name, outs, in_specs, scratch=(), limit=8, flops=0, nbytes=0):
    shapes = [jax.ShapeDtypeStruct(shape, dtype) for shape, dtype in outs]
    return pl.pallas_call(
        kernel,
        name=name,
        out_shape=shapes,
        in_specs=in_specs,
        out_specs=[VMEM] * len(shapes),
        scratch_shapes=list(scratch),
        compiler_params=pltpu.CompilerParams(vmem_limit_bytes=limit << 20),
        cost_estimate=pl.CostEstimate(flops=flops, bytes_accessed=nbytes, transcendentals=0),
    )


def shift(values, axis, step):
    size = lax.axis_size(axis)
    return lax.ppermute(values, axis, [(i, (i + step) % size) for i in range(size)])


def after(values, *others):
    return lax.optimization_barrier((values,) + others)[0]


def tables(session_row, owner_row):
    session_range = jnp.arange(SESS, dtype=jnp.int32)
    member = (session_row[:, None] == session_range[None, :]).astype(jnp.int32)
    counts = jnp.sum(member, axis=0)
    before = (session_row[None, :] < session_range[:, None]).astype(jnp.int32)
    starts = jnp.sum(before, axis=1)
    first_row = jnp.sum(member * starts[None, :], axis=1)
    position = jnp.arange(session_row.shape[0], dtype=jnp.int32) - first_row
    earlier = (owner_row[:, None] == owner_row[None, :]) & (
        session_range[None, :] < session_range[:, None]
    )
    owner_rank = jnp.sum(earlier.astype(jnp.int32), axis=1)
    owner_slot = owner_row * CAPS + owner_rank
    destination = jnp.sum(member * owner_slot[None, :], axis=1) * MOST + position
    return counts, session_row * ROOM + position, destination


def attention_kernel(
    spots, live, x0, t0, xl, tl, xr, tr, f1, f2, e1, e2, gain, wq, wk, wv, ck, cv, place,
    place_t, out, mine, xs, acc, slots, kk, vv, mixed, row_sem, cache_sem,
):
    half = f1.shape[0]
    copies = []
    for i, (ref, spot, extra) in enumerate(
        (
            (x0, 0, 0), (t0, 1, 0), (xl, 2, 0), (tl, 3, 0), (xr, 4, 0), (tr, 5, 0),
            (f1, 6, 0), (e1, 7, 0), (f2, 6, half), (e2, 7, half),
        )
    ):
        start = pl.multiple_of(spots[spot] + extra, 16)
        copies.append(
            pltpu.make_async_copy(ref, xs.at[pl.ds(start, ref.shape[0])], row_sem.at[i])
        )
    copies.append(pltpu.make_async_copy(ck, kk.at[:, pl.ds(0, CACHE)], cache_sem.at[0]))
    copies.append(pltpu.make_async_copy(cv, vv.at[:, pl.ds(0, CACHE)], cache_sem.at[1]))
    for copy in copies:
        copy.start()
    kk[:, CACHE + ROOM :, :] = jnp.zeros((SESS, KEYS - CACHE - ROOM, HEAD_DIM), jnp.bfloat16)
    vv[:, CACHE + ROOM :, :] = jnp.zeros((SESS, KEYS - CACHE - ROOM, HEAD_DIM), jnp.bfloat16)
    for copy in copies[:-2]:
        copy.wait()

    rows, width = xs.shape
    step = 512

    def square(i, total):
        x = xs[:, pl.ds(pl.multiple_of(i * step, step), step)].astype(jnp.float32)
        x = x * x
        for j in range(0, step, 128):
            total = total + x[:, j : j + 128]
        return total

    total = lax.fori_loop(0, width // step, square, jnp.zeros((rows, 128), jnp.float32))
    scale = lax.rsqrt(jnp.sum(total, axis=1, keepdims=True) / width + EPSILON)
    acc[...] = jnp.zeros_like(acc)
    heads = wq.shape[1]
    depth = 1024

    @pl.loop(0, width // depth)
    def _(i):
        part = pl.ds(pl.multiple_of(i * depth, depth), depth)
        x = xs[:, part].astype(jnp.float32) * scale * gain[:, part].astype(jnp.float32)
        x = x.astype(jnp.bfloat16)
        acc[:, :heads] += jnp.dot(x, wq[part, :], preferred_element_type=jnp.float32)
        acc[:, heads : heads + 128] += jnp.dot(
            x, wk[part, :], preferred_element_type=jnp.float32
        )
        acc[:, heads + 128 :] += jnp.dot(x, wv[part, :], preferred_element_type=jnp.float32)

    share = mine.shape[1]
    mine[...] = xs[:, pl.ds(pl.multiple_of(spots[8], share), share)]
    slots[...] = jnp.dot(
        place[...], acc[...].astype(jnp.bfloat16), preferred_element_type=jnp.float32
    ).astype(jnp.bfloat16)
    for copy in copies[-2:]:
        copy.wait()
    column = lax.broadcasted_iota(jnp.int32, (GQA * ROOM, KEYS), 1)
    place_in = lax.rem(lax.broadcasted_iota(jnp.int32, (GQA * ROOM, KEYS), 0), ROOM)
    fresh = column - CACHE
    allowed = (fresh >= 0) & (fresh <= place_in)
    fresh = jnp.where(allowed, fresh, KEYS)

    @pl.loop(0, SESS // 4)
    def _(group):
        for inner in range(4):
            s = group * 4 + inner
            at = pl.ds(pl.multiple_of(s * ROOM, ROOM), ROOM)
            kk[s, CACHE : CACHE + ROOM, :] = slots[at, heads : heads + 128]
            vv[s, CACHE : CACHE + ROOM, :] = slots[at, heads + 128 :]
            q = jnp.concatenate(
                [slots[at, h * HEAD_DIM : (h + 1) * HEAD_DIM] for h in range(GQA)], axis=0
            )
            scores = lax.dot_general(
                q, kk[s], (((1,), (1,)), ((), ())), preferred_element_type=jnp.float32
            ) * (HEAD_DIM ** (-0.5))
            keep = (column < live[0, s]) | (fresh < live[1, s])
            scores = jnp.where(keep, scores, -1e30)
            weights = jnp.exp(scores - jnp.max(scores, axis=1, keepdims=True))
            weights = weights / jnp.sum(weights, axis=1, keepdims=True)
            got = jnp.dot(
                weights.astype(jnp.bfloat16), vv[s], preferred_element_type=jnp.float32
            ).astype(jnp.bfloat16)
            for h in range(GQA):
                mixed[at, h * HEAD_DIM : (h + 1) * HEAD_DIM] = got[h * ROOM : (h + 1) * ROOM]

    out[...] = jnp.dot(place_t[...], mixed[...], preferred_element_type=jnp.float32).astype(
        jnp.bfloat16
    )


def block(values, weights, spot, width):
    return jnp.dot(
        values, weights[:, pl.ds(pl.multiple_of(spot, width), width)],
        preferred_element_type=jnp.float32,
    ).astype(jnp.bfloat16)


def far_kernel(spots, rows, w_out, send, keep):
    send[...] = block(rows[...], w_out, spots[0], send.shape[1])
    keep[...] = block(rows[...], w_out, spots[1], keep.shape[1])


def near_kernel(spots, rows, w_out, send, keep):
    @pl.loop(0, 3)
    def _(i):
        send[i] = block(rows[...], w_out, spots[2 + i], send.shape[2])
        keep[i] = block(rows[...], w_out, spots[5 + i], keep.shape[2])


def halves_kernel(keep, other, first, second):
    total = keep[...].astype(jnp.float32) + other[...].astype(jnp.float32)
    total = total.astype(jnp.bfloat16)
    half = first.shape[0]
    first[...] = total[:half]
    second[...] = total[half:]


def relay_kernel(keep, other, ahead, behind, to_next, to_last):
    half = ahead.shape[0]
    for i, ref, got, low in ((0, to_next, ahead, 0), (1, to_last, behind, half)):
        high = half - low
        first = keep[i].astype(jnp.float32) + other[i].astype(jnp.float32)
        ref[low : low + half] = (
            first[low : low + half] + got[...].astype(jnp.float32)
        ).astype(jnp.bfloat16)
        ref[high : high + half] = first[high : high + half].astype(jnp.bfloat16)


def split3(values):
    high = values.astype(jnp.bfloat16).astype(jnp.float32)
    rest = values - high
    middle = rest.astype(jnp.bfloat16).astype(jnp.float32)
    return high, middle, rest - middle


def talker_kernel(
    spots, mine, keep, other, from_last, from_next, gain, s0, sl, sr, g1, g2, send, kept,
    squares, wt, sem,
):
    piece = wt.shape[0] // 16
    copies = []
    for ref, source, first, number in ((s0, 0, 0, 4), (sl, 1, 0, 4), (sr, 2, 0, 4), (g1, 3, 0, 2), (g2, 3, 2, 2)):
        for j in range(number):
            start = pl.multiple_of(spots[8 + source * 4 + first + j], piece)
            copies.append(
                pltpu.make_async_copy(
                    ref.at[pl.ds(j * piece, piece)], wt.at[pl.ds(start, piece)], sem.at[len(copies)]
                )
            )
    for copy in copies:
        copy.start()
    total = (
        mine[...].astype(jnp.float32)
        + keep[2].astype(jnp.float32)
        + other[2].astype(jnp.float32)
        + from_last[...].astype(jnp.float32)
        + from_next[...].astype(jnp.float32)
    )
    hidden = total.astype(jnp.bfloat16).astype(jnp.float32)
    square = jnp.zeros((hidden.shape[0], 128), jnp.float32)
    for j in range(0, hidden.shape[1], 128):
        square = square + hidden[:, j : j + 128] * hidden[:, j : j + 128]
    row = jnp.sum(jnp.transpose(square), axis=0, keepdims=True)
    squares[...] = jnp.broadcast_to(row, squares.shape)
    share = hidden.shape[1]
    scaled = (hidden * gain[...].astype(jnp.float32)).astype(jnp.bfloat16)
    for copy in copies:
        copy.wait()
    rows, width = kept.shape
    kept[...] = jnp.dot(
        scaled, wt[:, pl.ds(pl.multiple_of(spots[24], width), width)],
        preferred_element_type=jnp.float32,
    )
    send[:rows] = jnp.dot(
        scaled, wt[:, pl.ds(pl.multiple_of(spots[25], width), width)],
        preferred_element_type=jnp.float32,
    ).astype(jnp.bfloat16)
    parts = jnp.concatenate(list(split3(row)) + [jnp.zeros((13, rows), jnp.float32)], axis=0)
    parts = jnp.concatenate([parts, jnp.zeros((16, width - rows), jnp.float32)], axis=1)
    send[rows:] = parts.astype(jnp.bfloat16)


def across_kernel(spots, kept, squares, got, own, squares_out, s1, s3, s2):
    rows = kept.shape[0]
    width = own.shape[1]
    tail = got[rows:, :rows].astype(jnp.float32)
    row = squares[0:1] + (tail[0:1] + tail[1:2] + tail[2:3])
    squares_out[...] = jnp.broadcast_to(row, squares_out.shape)
    pieces = []
    for part in split3(row):
        pieces += [part[:, j : j + 128] for j in range(0, rows, 128)]
    tail = jnp.concatenate(
        pieces + [jnp.zeros((16 - len(pieces), 128), jnp.float32)], axis=0
    ).astype(jnp.bfloat16)
    for i, ref in enumerate((own, s1, s3, s2)):
        at = pl.ds(pl.multiple_of(spots[26 + i], width), width)
        total = kept[:, at] + got[:rows, at].astype(jnp.float32)
        ref[:rows] = total.astype(ref.dtype)
        if i > 0:
            ref[rows:] = tail


def route_kernel(own, squares, g1, g3, g2, routing, out, *, features):
    rows = own.shape[0]
    total = own[...]
    row = squares[0:1]
    for ref in (g1, g3, g2):
        total = total + ref[:rows].astype(jnp.float32)
        tail = ref[rows:].astype(jnp.float32)
        row = row + jnp.concatenate(
            [tail[j : j + 1] + tail[2 + j : 3 + j] + tail[4 + j : 5 + j] for j in range(2)], axis=1
        )
    scale = lax.rsqrt(row / features + EPSILON)
    scale = jnp.transpose(jnp.broadcast_to(scale, (128, rows)))
    values = (total * scale).astype(jnp.bfloat16)
    out[...] = jnp.dot(routing[...], values, preferred_element_type=jnp.float32).astype(
        jnp.bfloat16
    )


def talker_strip(w_talker):
    y, core = lax.axis_index("y"), lax.axis_index("core")
    group = lax.axis_index("x") * 4 + lax.axis_index("z")
    width = w_talker.shape[1]
    piece = w_talker.shape[0] // 128
    mine = lax.dynamic_index_in_dim(
        w_talker.reshape(4, 2, 16, piece, width), group, 2, keepdims=False
    )
    kept = lax.dynamic_index_in_dim(mine, core, 1, keepdims=False)
    twin = shift(lax.dynamic_index_in_dim(mine, 1 - core, 1, keepdims=False), "core", 1)
    both = jnp.where(core == 0, jnp.stack([kept, twin], 1), jnp.stack([twin, kept], 1))
    across = jnp.zeros((4, 2, piece, width), w_talker.dtype)
    for d in (0, 1, 3, 2):
        part = lax.dynamic_index_in_dim(both, (y + d) % 4, 0, keepdims=False)
        part = part if d == 0 else shift(part, "y", d)
        across = lax.dynamic_update_index_in_dim(across, part, (y - d) % 4, 0)
    return jnp.transpose(across, (2, 1, 0, 3)).reshape(piece, 8 * width)


def on_device(
    thinker_rows,
    norm_gain,
    w_query,
    w_key,
    w_value,
    w_out,
    cache_keys,
    cache_values,
    session_ids,
    cache_lens,
    owners,
    talker_gain,
    w_talker,
):
    local, features = thinker_rows.shape
    bf16, f32 = jnp.bfloat16, jnp.float32
    tokens = local * 8
    share = features // 8
    width = w_talker.shape[1]
    heads = w_query.shape[1]
    x, z = lax.axis_index("x"), lax.axis_index("z")
    y, core = lax.axis_index("y"), lax.axis_index("core")
    member = y * 2 + core
    near = [y, (y + 3) % 4, (y + 1) % 4, (y + 2) % 4]
    counts, slot, destination = tables(session_ids[0], owners[:, 0])
    place_t = (slot[:, None] == jnp.arange(SESS * ROOM, dtype=jnp.int32)[None, :]).astype(bf16)
    place = (slot[None, :] == jnp.arange(SESS * ROOM, dtype=jnp.int32)[:, None]).astype(bf16)
    routing = (
        destination[None, :] == jnp.arange(16 * CAPS * MOST, dtype=jnp.int32)[:, None]
    ).astype(bf16)
    live = jnp.stack([cache_lens[0], counts])
    row_spots = []
    for chip in near:
        row_spots += [(chip * 2 + core) * local, (chip * 2 + 1 - core) * local]
    row_spots = jnp.stack(row_spots + [member * share]).astype(jnp.int32)
    order = [(y + 2) % 4, (y + 1) % 4, (y + 3) % 4, y]
    sends = [(chip * 2 + 1 - core) * share for chip in order]
    keeps = [(chip * 2 + core) * share for chip in order]
    column_spots = jnp.stack([sends[0], keeps[0]] + sends[1:] + keeps[1:])
    nearx = [x, (x + 3) % 4, (x + 1) % 4, (x + 2) % 4]
    nearz = [z, (z + 3) % 4, (z + 1) % 4, (z + 2) % 4]
    piece = share // 16
    row_of = [(cx * 4 + cz) * piece for cx in nearx for cz in nearz]
    rest = [core * 4 * width, (1 - core) * 4 * width]
    rest += [((y + d) % 4) * width for d in (0, 1, 3, 2)]
    spots = jnp.concatenate([column_spots, jnp.stack(row_of + rest)]).astype(jnp.int32)
    gain = lax.dynamic_slice(talker_gain, (member * share,), (share,))[None, :]

    half = local // 2
    left, right = shift(thinker_rows, "y", 1), shift(thinker_rows, "y", -1)
    twin = shift(thinker_rows, "core", 1)
    strip = talker_strip(w_talker)
    low, high = left[:half], right[half:]
    far_low, far_high = shift(low, "y", 1), shift(high, "y", -1)
    twin_left, twin_right = shift(left, "core", 1), shift(right, "core", 1)
    twin_low, twin_high = shift(far_low, "core", 1), shift(far_high, "core", 1)
    strip = after(strip, left, right)
    strips = [strip] + [shift(strip, "z", d) for d in (1, 3, 2)]

    rows, mine = call(
        attention_kernel,
        "attention",
        [((tokens, heads), bf16), ((tokens, share), bf16)],
        [SMEM, SMEM] + [ANY] * 10 + [VMEM] * 4 + [ANY] * 2 + [VMEM] * 2,
        [
            pltpu.VMEM((tokens, features), bf16),
            pltpu.VMEM((tokens, heads + 256), f32),
            pltpu.VMEM((SESS * ROOM, heads + 256), bf16),
            pltpu.VMEM((SESS, KEYS, HEAD_DIM), bf16),
            pltpu.VMEM((SESS, KEYS, HEAD_DIM), bf16),
            pltpu.VMEM((SESS * ROOM, heads), bf16),
            pltpu.SemaphoreType.DMA((10,)),
            pltpu.SemaphoreType.DMA((2,)),
        ],
        limit=20,
        flops=4 * 10**9,
        nbytes=20 * 10**6,
    )(
        row_spots, live, thinker_rows, twin, left, twin_left, right, twin_right, far_low,
        far_high, twin_low, twin_high, norm_gain[None, :], w_query, w_key, w_value, cache_keys,
        cache_values, place, place_t,
    )
    block_type = ((tokens, share), bf16)
    send_far, keep_far = call(
        far_kernel, "out_far", [block_type] * 2, [SMEM, VMEM, VMEM], flops=5 * 10**8, nbytes=4 * 10**6
    )(spots, rows, w_out)
    other_far = shift(send_far, "core", 1)
    send, keep = call(
        near_kernel, "out_near", [((3, tokens, share), bf16)] * 2, [SMEM, VMEM, VMEM],
        flops=15 * 10**8, nbytes=8 * 10**6,
    )(spots, rows, w_out)
    first, second = call(
        halves_kernel, "halves", [((tokens // 2, share), bf16)] * 2, [VMEM] * 2,
        flops=10**6, nbytes=2 * 10**6,
    )(keep_far, other_far)
    ahead, behind = shift(first, "y", 1), shift(second, "y", -1)
    other = shift(send, "core", 1)
    strip = after(jnp.concatenate(strips, 0), first)
    strip_left, strip_right = shift(strip, "x", 1), shift(strip, "x", -1)
    to_next, to_last = call(
        relay_kernel, "relay", [block_type] * 2, [VMEM] * 4, flops=10**6, nbytes=4 * 10**6
    )(keep, other, ahead, behind)
    from_last, from_next = shift(to_next, "y", 1), shift(to_last, "y", -1)
    strip_half = strip.shape[0] // 2
    strip_low = shift(after(strip_left[:strip_half], to_next), "x", 1)
    strip_high = shift(after(strip_right[strip_half:], to_next), "x", -1)
    sent, kept, squares = call(
        talker_kernel,
        "talker",
        [((tokens + 16, 4 * width), bf16), ((tokens, 4 * width), f32), ((8, tokens), f32)],
        [SMEM] + [VMEM] * 6 + [ANY] * 5,
        [pltpu.VMEM((share, 8 * width), bf16), pltpu.SemaphoreType.DMA((16,))],
        flops=6 * 10**8,
        nbytes=4 * 10**6,
    )(
        spots, mine, keep, other, from_last, from_next, gain, strip, strip_left, strip_right,
        strip_low, strip_high,
    )
    got = shift(sent, "core", 1)
    tall = ((tokens + 16, width), bf16)
    own, squares, s1, s3, s2 = call(
        across_kernel, "across", [((tokens, width), f32), ((8, tokens), f32), tall, tall, tall],
        [SMEM] + [VMEM] * 3, flops=10**6, nbytes=10**6,
    )(spots, kept, squares, got)
    g2 = shift(s2, "y", 2)
    g1, g3 = shift(s1, "y", 1), shift(s3, "y", 3)
    (outgoing,) = call(
        functools.partial(route_kernel, features=features), "route",
        [((16 * CAPS * MOST, width), bf16)], [VMEM] * 6, flops=4 * 10**7, nbytes=10**6,
    )(own, squares, g1, g3, g2, routing)
    arrived = lax.all_to_all(
        outgoing.reshape(16, CAPS * MOST, width), ("x", "z"), split_axis=0, concat_axis=0, tiled=True
    )
    return arrived.reshape(16 * CAPS * MOST, width)


def solution(mesh):
    grp, tp = ("x", "z"), ("y", "core")
    return jax.shard_map(
        on_device,
        mesh=Mesh(mesh.devices.reshape(4, 4, 4, 2), grp + tp),
        in_specs=(
            P(grp + tp, None),
            P(),
            P(None, tp),
            P(None, tp),
            P(None, tp),
            P(tp, None),
            P(grp, None, tp),
            P(grp, None, tp),
            P(grp, None),
            P(grp, None),
            P(grp, None),
            P(),
            P(None, tp),
        ),
        out_specs=P(grp, tp),
        check_vma=False,
    )
```

```python
import functools

import jax
import jax.numpy as jnp
from jax import lax
from jax.experimental import pallas as pl
from jax.experimental.pallas import tpu as pltpu
from jax.sharding import Mesh, PartitionSpec as P

HEAD_DIM = 128
SESS = 16
CACHE = 320
CAPS = 2
GQA = 4
MOST = 20
ROOM = 24
KEYS = 384

EPSILON = 1e-06

VMEM = pl.BlockSpec(memory_space=pltpu.VMEM)
SMEM = pl.BlockSpec(memory_space=pltpu.SMEM)
ANY = pl.BlockSpec(memory_space=pl.ANY)
DMA = pltpu.SemaphoreType.DMA


def call(kernel, outs, in_specs, scratch=(), limit=10, flops=0, nbytes=0):
    shapes = [jax.ShapeDtypeStruct(out[0], out[1]) for out in outs]
    return pl.pallas_call(
        kernel,
        out_shape=shapes,
        in_specs=in_specs,
        out_specs=[out[2] if len(out) > 2 else VMEM for out in outs],
        scratch_shapes=list(scratch),
        compiler_params=pltpu.CompilerParams(vmem_limit_bytes=limit << 20),
        cost_estimate=pl.CostEstimate(flops=flops, bytes_accessed=nbytes, transcendentals=0),
    )


def shift(values, axis, step):
    size = lax.axis_size(axis)
    return lax.ppermute(values, axis, [(i, (i + step) % size) for i in range(size)])


def tables(session_row, owner_row):
    session_range = jnp.arange(SESS, dtype=jnp.int32)
    member = (session_row[:, None] == session_range[None, :]).astype(jnp.int32)
    before = (session_row[None, :] < session_range[:, None]).astype(jnp.int32)
    starts = jnp.sum(before, axis=1)
    first_row = jnp.sum(member * starts[None, :], axis=1)
    position = jnp.arange(session_row.shape[0], dtype=jnp.int32) - first_row
    earlier = (owner_row[:, None] == owner_row[None, :]) & (
        session_range[None, :] < session_range[:, None]
    )
    owner_rank = jnp.sum(earlier.astype(jnp.int32), axis=1)
    owner_slot = owner_row * CAPS + owner_rank
    destination = jnp.sum(member * owner_slot[None, :], axis=1) * MOST + position
    return session_row * ROOM + position, destination


def block(values, weights):
    return jnp.dot(values, weights[...], preferred_element_type=jnp.float32).astype(jnp.bfloat16)


def columns(ref, spot, width):
    return ref.at[:, pl.ds(pl.multiple_of(spot, width), width)]


def attention_kernel(
    spots, live, x0, t0, xl, tl, xr, tr, f1, f2, e1, e2, gain, wq, wk, wv, ck, cv, w_out, place,
    place_t, out, mine, send, keep, xs, ws, wo, acc, slots, kk, vv, mixed, row_sem, w_sem, sem,
):
    half = f1.shape[0]
    rows, width = xs.shape
    heads = wq.shape[1]
    share = mine.shape[1]
    depth = 1024
    row_copies = []
    for i, (ref, spot, extra) in enumerate(
        (
            (x0, 0, 0), (t0, 1, 0), (xl, 2, 0), (tl, 3, 0), (xr, 4, 0), (tr, 5, 0),
            (f1, 6, 0), (e1, 7, 0), (f2, 6, half), (e2, 7, half),
        )
    ):
        start = pl.multiple_of(spots[spot] + extra, 16)
        row_copies.append(
            pltpu.make_async_copy(ref, xs.at[pl.ds(start, ref.shape[0])], row_sem.at[i])
        )

    def weight_copies(i):
        part = pl.ds(pl.multiple_of(i * depth, depth), depth)
        return [
            pltpu.make_async_copy(
                ref.at[part], ws.at[part, pl.ds(low, ref.shape[1])], w_sem.at[j, i]
            )
            for j, (ref, low) in enumerate(((wq, 0), (wk, heads), (wv, heads + 128)))
        ]

    cache_copies = [
        pltpu.make_async_copy(ck, kk.at[:, pl.ds(0, CACHE)], sem.at[0]),
        pltpu.make_async_copy(cv, vv.at[:, pl.ds(0, CACHE)], sem.at[1]),
    ]
    out_copies = [
        pltpu.make_async_copy(columns(w_out, spots[9 + i], share), wo.at[i], sem.at[2 + i])
        for i in range(2)
    ]
    for copy in row_copies:
        copy.start()
    for i in range(width // depth):
        for copy in weight_copies(i):
            copy.start()
    for copy in cache_copies + out_copies:
        copy.start()
    unused = jnp.zeros((SESS, KEYS - CACHE - ROOM, HEAD_DIM), jnp.bfloat16)
    kk[:, CACHE + ROOM :, :] = unused
    vv[:, CACHE + ROOM :, :] = unused
    for copy in row_copies:
        copy.wait()
    mine_copy = pltpu.make_async_copy(columns(xs, spots[8], share), mine, sem.at[4])
    mine_copy.start()
    step = 512

    def square(i, total):
        x = xs[:, pl.ds(pl.multiple_of(i * step, step), step)].astype(jnp.float32)
        x = x * x
        for j in range(0, step, 128):
            total = total + x[:, j : j + 128]
        return total

    total = lax.fori_loop(0, width // step, square, jnp.zeros((rows, 128), jnp.float32))
    scale = lax.rsqrt(jnp.sum(total, axis=1, keepdims=True) / width + EPSILON)
    acc[...] = jnp.zeros_like(acc)

    @pl.loop(0, width // depth)
    def _(i):
        part = pl.ds(pl.multiple_of(i * depth, depth), depth)
        x = xs[:, part].astype(jnp.float32) * scale * gain[:, part].astype(jnp.float32)
        for copy in weight_copies(i):
            copy.wait()
        acc[...] += jnp.dot(
            x.astype(jnp.bfloat16), ws[part, :], preferred_element_type=jnp.float32
        )

    slots[...] = jnp.dot(
        place[...], acc[...].astype(jnp.bfloat16), preferred_element_type=jnp.float32
    )
    for copy in cache_copies:
        copy.wait()
    new_keys = slots[:, heads : heads + 128].reshape(SESS, ROOM, HEAD_DIM)
    new_values = slots[:, heads + 128 :].reshape(SESS, ROOM, HEAD_DIM)
    kk[:, CACHE : CACHE + ROOM, :] = new_keys.astype(jnp.bfloat16)
    vv[:, CACHE : CACHE + ROOM, :] = new_values.astype(jnp.bfloat16)
    column = lax.broadcasted_iota(jnp.int32, (GQA * ROOM, KEYS), 1)
    place_in = lax.rem(lax.broadcasted_iota(jnp.int32, (GQA * ROOM, KEYS), 0), ROOM)
    fresh = column - CACHE
    causal = (fresh <= place_in) & (fresh < ROOM)
    column = jnp.where(fresh < 0, column, jnp.where(causal, -1, CACHE))
    together = 4

    @pl.loop(0, SESS // together)
    def _(group):
        first = group * together
        spans = [pl.ds(pl.multiple_of((first + i) * ROOM, 8), ROOM) for i in range(together)]
        queries = [
            jnp.concatenate(
                [slots[at, h * HEAD_DIM : (h + 1) * HEAD_DIM] for h in range(GQA)], axis=0
            ).astype(jnp.bfloat16)
            for at in spans
        ]
        scores = [
            lax.dot_general(
                queries[i], kk[first + i], (((1,), (1,)), ((), ())),
                preferred_element_type=jnp.float32,
            )
            for i in range(together)
        ]
        results = []
        for i in range(together):
            score = jnp.where(
                column < live[0, first + i], scores[i] * (HEAD_DIM ** (-0.5)), -1e30
            )
            weights = jnp.exp(score - jnp.max(score, axis=1, keepdims=True))
            weights = weights * (1.0 / jnp.sum(weights, axis=1, keepdims=True))
            results.append(
                jnp.dot(
                    weights.astype(jnp.bfloat16), vv[first + i],
                    preferred_element_type=jnp.float32,
                )
            )
        for at, got in zip(spans, results):
            for h in range(GQA):
                mixed[at, h * HEAD_DIM : (h + 1) * HEAD_DIM] = got[h * ROOM : (h + 1) * ROOM]

    attended = jnp.dot(
        place_t[...], mixed[...].astype(jnp.bfloat16), preferred_element_type=jnp.float32
    ).astype(jnp.bfloat16)
    out[...] = attended
    for copy in out_copies:
        copy.wait()
    send[...] = block(attended, wo.at[0])
    keep[...] = block(attended, wo.at[1])
    mine_copy.wait()


def project_kernel(spots, rows, w_out, out, wo, sem, *, first):
    copies = [
        pltpu.make_async_copy(columns(w_out, spots[first + i], wo.shape[2]), wo.at[i], sem.at[i])
        for i in range(3)
    ]
    for copy in copies:
        copy.start()
    for i in range(3):
        copies[i].wait()
        out[i] = block(rows[...], wo.at[i])


def halves_kernel(keep, other, first, second):
    total = keep[...].astype(jnp.float32) + other[...].astype(jnp.float32)
    total = total.astype(jnp.bfloat16)
    half = first.shape[0]
    first[...] = total[:half]
    second[...] = total[half:]


def pack_kernel(s0, s1, s3, s2, out, sem):
    copies = [
        pltpu.make_async_copy(ref, out.at[i], sem.at[i]) for i, ref in enumerate((s0, s1, s3, s2))
    ]
    for copy in copies:
        copy.start()
    for copy in copies:
        copy.wait()


def fetch(pairs, sem):
    copies = [pltpu.make_async_copy(ref, buf, sem.at[i]) for i, (ref, buf) in enumerate(pairs)]
    for copy in copies:
        copy.start()
    return copies


def relay_kernel(keep, other, ahead, behind, to_next, to_last, kb, ob, ab, bb, sem):
    half = ahead.shape[0]
    pairs = []
    for i, (got, buf) in enumerate(((ahead, ab), (behind, bb))):
        pairs += [(keep.at[i], kb.at[i]), (other.at[i], ob.at[i]), (got, buf)]
    copies = fetch(pairs, sem)
    for i, (ref, got, low) in enumerate(((to_next, ab, 0), (to_last, bb, half))):
        for copy in copies[3 * i : 3 * i + 3]:
            copy.wait()
        high = half - low
        total = kb[i].astype(jnp.float32) + ob[i].astype(jnp.float32)
        ref[low : low + half] = (
            total[low : low + half] + got[...].astype(jnp.float32)
        ).astype(jnp.bfloat16)
        ref[high : high + half] = total[high : high + half].astype(jnp.bfloat16)


def split3(values):
    high = values.astype(jnp.bfloat16).astype(jnp.float32)
    rest = values - high
    middle = rest.astype(jnp.bfloat16).astype(jnp.float32)
    return high, middle, rest - middle


def prepare_kernel(
    spots, mine, keep, other, s0, sl, sr, g1, g2, base, weights, mb, kb, ob, wt, sem
):
    piece = s0.shape[2]
    copies = fetch([(mine, mb), (keep.at[2], kb), (other.at[2], ob)], sem)
    pieces = []
    for ref, source, first, number in (
        (s0, 0, 0, 4), (sl, 1, 0, 4), (sr, 2, 0, 4), (g1, 3, 0, 2), (g2, 3, 2, 2),
    ):
        for j in range(number):
            start = pl.multiple_of(spots[11 + source * 4 + first + j], piece)
            pieces.append(
                pltpu.make_async_copy(
                    ref.at[j], wt.at[:, pl.ds(start, piece)], sem.at[3 + len(pieces)]
                )
            )
            pieces[-1].start()
    for copy in copies:
        copy.wait()
    base[...] = (
        mb[...].astype(jnp.float32) + kb[...].astype(jnp.float32) + ob[...].astype(jnp.float32)
    )
    for copy in pieces:
        copy.wait()
    width = wt.shape[2]
    for source in range(8):
        at = (source % 2 * 4 + source // 2) * width
        weights[:, at : at + width] = wt[source]


def talker_kernel(
    spots, base, from_last, from_next, gain, weights, send, kept, squares, bb, lb, nb, wb, sem
):
    copies = fetch([(base, bb), (from_last, lb), (from_next, nb), (weights, wb)], sem)
    for copy in copies[:3]:
        copy.wait()
    total = bb[...] + lb[...].astype(jnp.float32) + nb[...].astype(jnp.float32)
    hidden = total.astype(jnp.bfloat16).astype(jnp.float32)
    square = jnp.zeros((hidden.shape[0], 128), jnp.float32)
    for j in range(0, hidden.shape[1], 128):
        square = square + hidden[:, j : j + 128] * hidden[:, j : j + 128]
    row = jnp.sum(jnp.transpose(square), axis=0, keepdims=True)
    squares[...] = jnp.broadcast_to(row, squares.shape)
    scaled = (hidden * gain[...].astype(jnp.float32)).astype(jnp.bfloat16)
    rows, width = kept.shape
    copies[3].wait()
    send[:rows] = jnp.dot(
        scaled, wb[:, pl.ds(pl.multiple_of(spots[28], width), width)],
        preferred_element_type=jnp.float32,
    ).astype(jnp.bfloat16)
    kept[...] = jnp.dot(
        scaled, wb[:, pl.ds(pl.multiple_of(spots[27], width), width)],
        preferred_element_type=jnp.float32,
    )
    parts = jnp.concatenate(list(split3(row)) + [jnp.zeros((13, rows), jnp.float32)], axis=0)
    parts = jnp.concatenate([parts, jnp.zeros((16, width - rows), jnp.float32)], axis=1)
    send[rows:] = parts.astype(jnp.bfloat16)


def across_kernel(spots, kept, squares, got, own, squares_out, s1, s3, s2):
    rows = kept.shape[0]
    width = own.shape[1]
    tail = got[rows:, :rows].astype(jnp.float32)
    row = squares[0:1] + (tail[0:1] + tail[1:2] + tail[2:3])
    squares_out[...] = jnp.broadcast_to(row, squares_out.shape)
    pieces = []
    for part in split3(row):
        pieces += [part[:, j : j + 128] for j in range(0, rows, 128)]
    tail = jnp.concatenate(
        pieces + [jnp.zeros((16 - len(pieces), 128), jnp.float32)], axis=0
    ).astype(jnp.bfloat16)
    for i, ref in enumerate((own, s1, s3, s2)):
        at = pl.ds(pl.multiple_of(spots[29 + i], width), width)
        total = kept[:, at] + got[:rows, at].astype(jnp.float32)
        ref[:rows] = total.astype(ref.dtype)
        if i > 0:
            ref[rows:] = tail


def route_kernel(own, squares, g1, g3, g2, routing, out, *, features):
    rows = own.shape[0]
    total = own[...]
    row = squares[0:1]
    for ref in (g1, g3, g2):
        total = total + ref[:rows].astype(jnp.float32)
        tail = ref[rows:].astype(jnp.float32)
        row = row + jnp.concatenate(
            [tail[j : j + 1] + tail[2 + j : 3 + j] + tail[4 + j : 5 + j] for j in range(2)], axis=1
        )
    scale = lax.rsqrt(row / features + EPSILON)
    scale = jnp.transpose(jnp.broadcast_to(scale, (128, rows)))
    values = (total * scale).astype(jnp.bfloat16)
    out[...] = jnp.dot(routing[...], values, preferred_element_type=jnp.float32).astype(
        jnp.bfloat16
    )


def on_device(
    thinker_rows,
    norm_gain,
    w_query,
    w_key,
    w_value,
    w_out,
    cache_keys,
    cache_values,
    session_ids,
    cache_lens,
    owners,
    talker_gain,
    w_talker,
):
    local, features = thinker_rows.shape
    bf16, f32 = jnp.bfloat16, jnp.float32
    tokens = local * 8
    share = features // 8
    width = w_talker.shape[1]
    heads = w_query.shape[1]
    piece = share // 16
    x, z = lax.axis_index("x"), lax.axis_index("z")
    y, core = lax.axis_index("y"), lax.axis_index("core")
    member = y * 2 + core

    half = local // 2
    left, right = shift(thinker_rows, "y", 1), shift(thinker_rows, "y", -1)
    twin = shift(thinker_rows, "core", 1)
    strip = lax.dynamic_index_in_dim(
        w_talker.reshape(8, 16, piece, width), x * 4 + z, 1, keepdims=False
    )
    strip = lax.all_to_all(strip, ("y", "core"), split_axis=0, concat_axis=0, tiled=True)
    left, right, strip = lax.optimization_barrier((left, right, strip))
    low, high = left[:half], right[half:]
    far_low, far_high = shift(low, "y", 1), shift(high, "y", -1)
    twin_left, twin_right = shift(left, "core", 1), shift(right, "core", 1)
    strips = [strip] + [shift(strip, "z", d) for d in (1, 3, 2)]
    twin_low, twin_high = shift(far_low, "core", 1), shift(far_high, "core", 1)

    near = [y, (y + 3) % 4, (y + 1) % 4, (y + 2) % 4]
    ids, lens, owner_ids, _ = lax.optimization_barrier((session_ids, cache_lens, owners, left))
    slot, destination = tables(ids[0], owner_ids[:, 0])
    places = jnp.arange(SESS * ROOM, dtype=jnp.int32)
    place_t = (slot[:, None] == places[None, :]).astype(bf16)
    place = (slot[None, :] == places[:, None]).astype(bf16)
    routing = (
        destination[None, :] == jnp.arange(16 * CAPS * MOST, dtype=jnp.int32)[:, None]
    ).astype(bf16)
    spots = []
    for chip in near:
        spots += [(chip * 2 + core) * local, (chip * 2 + 1 - core) * local]
    spots += [member * share]
    order = [(y + 2) % 4, (y + 1) % 4, (y + 3) % 4, y]
    sends = [(chip * 2 + 1 - core) * share for chip in order]
    keeps = [(chip * 2 + core) * share for chip in order]
    nearx = [x, (x + 3) % 4, (x + 1) % 4, (x + 2) % 4]
    nearz = [z, (z + 3) % 4, (z + 1) % 4, (z + 2) % 4]
    spots += [sends[0], keeps[0]]
    spots += [(cx * 4 + cz) * piece for cx in nearx for cz in nearz]
    spots += [core * 4 * width, (1 - core) * 4 * width]
    spots += [((y + d) % 4) * width for d in (0, 1, 3, 2)]
    spots = jnp.stack(spots + sends[1:] + keeps[1:]).astype(jnp.int32)
    gain = lax.dynamic_slice(talker_gain, (member * share,), (share,))[None, :]

    block_type = ((tokens, share), bf16)
    rows, mine, send_far, keep_far = call(
        attention_kernel,
        [((tokens, heads), bf16), block_type + (ANY,), block_type, block_type],
        [SMEM, SMEM] + [ANY] * 10 + [VMEM] + [ANY] * 6 + [VMEM] * 2,
        [
            pltpu.VMEM((tokens, features), bf16),
            pltpu.VMEM((features, heads + 256), bf16),
            pltpu.VMEM((2, heads, share), bf16),
            pltpu.VMEM((tokens, heads + 256), f32),
            pltpu.VMEM((SESS * ROOM, heads + 256), f32),
            pltpu.VMEM((SESS, KEYS, HEAD_DIM), bf16),
            pltpu.VMEM((SESS, KEYS, HEAD_DIM), bf16),
            pltpu.VMEM((SESS * ROOM, heads), f32),
            DMA((10,)),
            DMA((3, 8)),
            DMA((5,)),
        ],
        limit=36,
        flops=5 * 10**9,
        nbytes=24 * 10**6,
    )(
        spots, lens, thinker_rows, twin, left, twin_left, right, twin_right, far_low,
        far_high, twin_low, twin_high, norm_gain[None, :], w_query, w_key, w_value, cache_keys,
        cache_values, w_out, place, place_t,
    )
    other_far = shift(send_far, "core", 1)

    def project(first):
        return call(
            functools.partial(project_kernel, first=first),
            [((3, tokens, share), bf16)],
            [SMEM, VMEM, ANY],
            [pltpu.VMEM((3, heads, share), bf16), DMA((3,))],
            flops=8 * 10**8,
            nbytes=5 * 10**6,
        )(spots, rows, w_out)[0]

    send = project(33)
    other = shift(send, "core", 1)
    first, second = call(
        halves_kernel, [((tokens // 2, share), bf16)] * 2, [VMEM] * 2,
        flops=10**6, nbytes=2 * 10**6,
    )(keep_far, other_far)
    ahead, behind = shift(first, "y", 1), shift(second, "y", -1)
    keep = project(36)
    (strip,) = call(
        pack_kernel, [((4, 8, piece, width), bf16, ANY)], [ANY] * 4, [DMA((4,))],
        flops=10**5, nbytes=10**6,
    )(*strips)
    strip_left, strip_right = shift(strip, "x", 1), shift(strip, "x", -1)
    to_next, to_last = call(
        relay_kernel,
        [block_type] * 2,
        [ANY] * 4,
        [pltpu.VMEM((2, tokens, share), bf16)] * 2
        + [pltpu.VMEM((tokens // 2, share), bf16)] * 2
        + [DMA((6,))],
        flops=10**6,
        nbytes=4 * 10**6,
    )(keep, other, ahead, behind)
    from_last, from_next = shift(to_next, "y", 1), shift(to_last, "y", -1)
    strip_low = shift(strip_left[:2], "x", 1)
    strip_high = shift(strip_right[2:], "x", -1)
    base, weights = call(
        prepare_kernel,
        [((tokens, share), f32), ((share, 8 * width), bf16)],
        [SMEM] + [ANY] * 8,
        [pltpu.VMEM((tokens, share), bf16)] * 3
        + [pltpu.VMEM((8, share, width), bf16), DMA((19,))],
        flops=10**6,
        nbytes=4 * 10**6,
    )(spots, mine, keep, other, strip, strip_left, strip_right, strip_low, strip_high)
    sent, kept, squares = call(
        talker_kernel,
        [((tokens + 16, 4 * width), bf16), ((tokens, 4 * width), f32), ((8, tokens), f32)],
        [SMEM] + [ANY] * 3 + [VMEM, ANY],
        [pltpu.VMEM((tokens, share), f32)]
        + [pltpu.VMEM((tokens, share), bf16)] * 2
        + [pltpu.VMEM((share, 8 * width), bf16), DMA((4,))],
        flops=6 * 10**8,
        nbytes=4 * 10**6,
    )(spots, base, from_last, from_next, gain, weights)
    got = shift(sent, "core", 1)
    tall = ((tokens + 16, width), bf16)
    own, squares, s1, s3, s2 = call(
        across_kernel, [((tokens, width), f32), ((8, tokens), f32), tall, tall, tall],
        [SMEM] + [VMEM] * 3, flops=10**6, nbytes=10**6,
    )(spots, kept, squares, got)
    g2 = shift(s2, "y", 2)
    g1, g3 = shift(s1, "y", 1), shift(s3, "y", 3)
    (outgoing,) = call(
        functools.partial(route_kernel, features=features),
        [((16 * CAPS * MOST, width), bf16)], [VMEM] * 6, flops=4 * 10**7, nbytes=10**6,
    )(own, squares, g1, g3, g2, routing)
    arrived = lax.all_to_all(
        outgoing.reshape(16, CAPS * MOST, width), ("x", "z"), split_axis=0, concat_axis=0,
        tiled=True,
    )
    return arrived.reshape(16 * CAPS * MOST, width)


def solution(mesh):
    grp, tp = ("x", "z"), ("y", "core")
    return jax.shard_map(
        on_device,
        mesh=Mesh(mesh.devices.reshape(4, 4, 4, 2), grp + tp),
        in_specs=(
            P(grp + tp, None),
            P(),
            P(None, tp),
            P(None, tp),
            P(None, tp),
            P(tp, None),
            P(grp, None, tp),
            P(grp, None, tp),
            P(grp, None),
            P(grp, None),
            P(grp, None),
            P(),
            P(None, tp),
        ),
        out_specs=P(grp, tp),
        check_vma=False,
    )
```
